256 devices in a mesh: tm: 16 (over y, x), space: 16 (over z, core).
Axes of the slice: x: 4, y: 4, z: 8, core: 2. Of those that a mesh axis runs over, the one named last changes fastest.
Arguments:
- queries: bfloat16 [98304, 2048], P(('tm', 'space')), may hold values from -8 to 8, as said below
- keys: bfloat16 [98304, 2048], P(('tm', 'space')), may hold values from -8 to 8, as said below
- values: bfloat16 [98304, 2048], P(('tm', 'space')), may hold values from -8 to 8, as said below
- cotangent: bfloat16 [98304, 2048], P(('tm', 'space')), may hold values from -8 to 8, as said below
Outputs:
- attended: bfloat16 [98304, 2048], P(('tm', 'space'))
- grad_queries: bfloat16 [98304, 2048], P(('tm', 'space'))
- grad_keys: bfloat16 [98304, 2048], P(('tm', 'space'))
- grad_values: bfloat16 [98304, 2048], P(('tm', 'space'))
The draws below stay inside these ranges and needn't reach their ends.
Inputs may be any that keep to these rules, and one draw needn't show every extreme that they name: `queries`: Real-valued activations. `keys`: Real-valued activations. `values`: Real-valued activations. `cotangent`: Real-valued cotangents.
All inputs are finite; a program needn't handle non-finite values.
Results may differ from the reference program's by a relative error of at most 0.008.
Values may be sent and summed in bfloat16 or wider, within the bound.
A program may use at most 128 MiB of HBM per device.

```python
import math
import jax
import jax.numpy as jnp
from jax import lax

HEADS = 16
HEAD_DIM = 128
TOK_DEV = 384
TOKENS = 98304
N_TM = 16
N_SPACE = 16


def blocky(seed_key, scale_lo, scale_hi, offset_amp):
    row_count = TOKENS
    col_count = HEADS * HEAD_DIM
    key_noise, key_scale, key_offset, key_column = jax.random.split(seed_key, 4)
    jitter = jax.random.normal(key_noise, (row_count, col_count), jnp.float32)
    row_scales = jnp.exp(jax.random.uniform(key_scale, (row_count, 1), jnp.float32, math.log(scale_lo), math.log(scale_hi)))
    col_scales = jnp.exp(jax.random.uniform(key_column, (1, col_count), jnp.float32, -0.5, 0.5))
    offsets = offset_amp * jax.random.normal(key_offset, (row_count // 32, 1, col_count), jnp.float32)
    offsets = jnp.broadcast_to(offsets, (row_count // 32, 32, col_count)).reshape(row_count, col_count)
    return jnp.clip(jitter * row_scales * col_scales + offsets, -8.0, 8.0).astype(jnp.bfloat16)


def draw_queries(key, part):
    return blocky(jax.random.fold_in(key, 11), 0.25, 2.5, 0.0)


def draw_keys(key, part):
    return blocky(jax.random.fold_in(key, 12), 0.25, 2.5, 0.0)


def draw_values(key, part):
    return blocky(jax.random.fold_in(key, 13), 0.3, 1.5, 0.3)


def draw_cotangent(key, part):
    return blocky(jax.random.fold_in(key, 14), 0.3, 1.5, 1.0)


def setup_inputs(seed: int = 0) -> dict:
    key_list = jax.random.split(jax.random.key(seed), 5)
    return {
        "queries": draw_queries(jax.random.fold_in(key_list[4], 71), 0),
        "keys": draw_keys(jax.random.fold_in(key_list[4], 71), 0),
        "values": draw_values(jax.random.fold_in(key_list[4], 71), 0),
        "cotangent": draw_cotangent(jax.random.fold_in(key_list[4], 71), 0),
    }


HIGH = lax.Precision.HIGHEST


def round_bfloat16_float32(array):
    return lax.optimization_barrier(array.astype(jnp.bfloat16)).astype(jnp.float32)


def reverse_cumsum(array):
    return jnp.flip(jnp.cumsum(jnp.flip(array, 0), axis=0), 0)


def reference(queries, keys, values, cotangent):
    group_len = TOK_DEV * N_SPACE
    shaped = (N_TM, group_len, HEADS, HEAD_DIM)
    query_all = queries.reshape(shaped)
    key_all = keys.reshape(shaped)
    value_all = values.reshape(shaped)
    grad_all = cotangent.reshape(shaped)

    def group_states(entry_list):
        block_keys, block_values = entry_list
        feat_k = jnp.maximum(block_keys.astype(jnp.float32), 0.0)
        value_f = block_values.astype(jnp.float32)
        return (jnp.einsum('thf,the->hfe', feat_k, value_f, precision=HIGH),
                jnp.sum(feat_k, axis=0), jnp.sum(value_f, axis=0))

    state_kv, key_sum, value_sum = lax.map(group_states, (key_all, value_all))
    prefix_kv = jnp.cumsum(state_kv, axis=0)
    prefix_ks = jnp.cumsum(key_sum, axis=0)
    prefix_vs = jnp.cumsum(value_sum, axis=0)
    counts = (jnp.arange(N_TM, dtype=jnp.float32) + 1.0) * group_len

    def forward_group(entry_list):
        query_block, grad_block, pkv, pks, pvs, count = entry_list
        feat_q = jnp.maximum(query_block.astype(jnp.float32), 0.0)
        prefix_round = round_bfloat16_float32(pkv)
        numer = jnp.einsum('thf,hfe->the', feat_q, prefix_round, precision=HIGH) + pvs[None]
        denom = jnp.einsum('thf,hf->th', feat_q, pks, precision=HIGH) + count
        attended = (numer / denom[..., None]).astype(jnp.bfloat16)
        grad_f = grad_block.astype(jnp.float32)
        dnum = grad_f / denom[..., None]
        dnum_round = round_bfloat16_float32(dnum)
        ratio = jnp.sum(grad_f * numer, axis=-1) / (denom * denom)
        d_feat = jnp.einsum('the,hfe->thf', dnum_round, prefix_round, precision=HIGH) - ratio[..., None] * pks[None]
        grad_q = jnp.where(query_block > 0, d_feat, 0.0).astype(jnp.bfloat16)
        back_kv = jnp.einsum('thf,the->hfe', feat_q, dnum_round, precision=HIGH)
        back_ks = -jnp.einsum('th,thf->hf', ratio, feat_q, precision=HIGH)
        back_vs = jnp.sum(dnum, axis=0)
        return attended, grad_q, back_kv, back_ks, back_vs

    attended, grad_q, back_kv, back_ks, back_vs = lax.map(
        forward_group, (query_all, grad_all, prefix_kv, prefix_ks, prefix_vs, counts))
    suffix_kv = reverse_cumsum(back_kv)
    suffix_ks = reverse_cumsum(back_ks)
    suffix_vs = reverse_cumsum(back_vs)

    def backward_group(entry_list):
        block_keys, block_values, suffix_key_value, suffix_key_sums, suffix_value_sums = entry_list
        feat_k = jnp.maximum(block_keys.astype(jnp.float32), 0.0)
        value_f = block_values.astype(jnp.float32)
        suffix_rounded = round_bfloat16_float32(suffix_key_value)
        grad_v = (jnp.einsum('thf,hfe->the', feat_k, suffix_rounded, precision=HIGH) + suffix_value_sums[None]).astype(jnp.bfloat16)
        d_key = jnp.einsum('the,hfe->thf', value_f, suffix_rounded, precision=HIGH) + suffix_key_sums[None]
        grad_k = jnp.where(block_keys > 0, d_key, 0.0).astype(jnp.bfloat16)
        return grad_k, grad_v

    grad_k, grad_v = lax.map(backward_group, (key_all, value_all, suffix_kv, suffix_ks, suffix_vs))
    flat = (TOKENS, HEADS * HEAD_DIM)
    return (attended.reshape(flat), grad_q.reshape(flat), grad_k.reshape(flat), grad_v.reshape(flat))
```

```python
import functools

import jax
import jax.numpy as jnp
from jax import lax
from jax.experimental import pallas as pl
from jax.experimental.pallas import tpu as pltpu
from jax.sharding import PartitionSpec as P

D = 128
STATE = D + 16
MESH = pl.DeviceIdType.MESH
F32 = jnp.float32
BF16 = jnp.bfloat16


def cols(head):
    return pl.ds(pl.multiple_of(head * D, D), D)


def sums_tile(key_row, value_row):
    row = lax.broadcasted_iota(jnp.int32, (16, D), 0)
    key_low = key_row - key_row.astype(BF16).astype(F32)
    value_low = value_row - value_row.astype(BF16).astype(F32)
    tile = jnp.where(row == 0, key_row, jnp.where(row == 1, key_low, 0.0))
    tile = jnp.where(row == 2, value_row, jnp.where(row == 3, value_low, tile))
    return tile.astype(BF16)


def split_sums(tile):
    return tile[0:1] + tile[1:2], tile[2:3] + tile[3:4]


def put_state(ref, matrix, key_row, value_row):
    ref[0:D, :] = matrix.astype(BF16)
    ref[D:STATE, :] = sums_tile(key_row, value_row)


def get_state(ref):
    return ref[...].astype(F32)


def put_packed(ref, packed):
    key_row, value_row = split_sums(packed[D:STATE])
    put_state(ref, packed[0:D], key_row, value_row)


def across(left, right):
    return lax.dot_general(left, right, (((0,), (0,)), ((), ())), preferred_element_type=F32)


def times(left, right):
    return jnp.dot(left, right, preferred_element_type=F32)


def times_t(left, right):
    return lax.dot_general(left, right, (((1,), (1,)), ((), ())), preferred_element_type=F32)


def kernel(
    sizes,
    q_hbm, k_hbm, v_hbm, g_hbm,
    att_hbm, gq_hbm, gk_hbm, gv_hbm,
    q_v, k_v, v_v, g_v, att_v, gq_v, gk_v, gv_v, dnum_v, ratio_v,
    own, pair_out, pair_in, z_out, z_in, x_out, x_in, y_out, y_in, total, fin,
    in_sem, out_sem, grad_sem,
    pair_ss, pair_rs, z_ss, z_rs, x_ss, x_rs, y_ss, y_rs, ag_ss, fw_ss, fin_rs,
):
    nx, ny, nz = sizes
    tm, space = lax.axis_index("tm"), lax.axis_index("space")
    y, x = lax.div(tm, nx), lax.rem(tm, nx)
    z, core = lax.div(space, 2), lax.rem(space, 2)
    partner = 2 * z + 1 - core
    rows = q_v.shape[0]

    def at_z(j):
        return 2 * j + core

    barrier = pltpu.get_barrier_semaphore()
    pl.semaphore_signal(barrier, inc=1, device_id={"space": partner}, device_id_type=MESH)
    for o in range(1, nz):
        pl.semaphore_signal(
            barrier, inc=1, device_id={"space": at_z(lax.rem(z + o, nz))}, device_id_type=MESH
        )
    for o in range(1, nx):
        pl.semaphore_signal(
            barrier, inc=1, device_id={"tm": y * nx + lax.rem(x + o, nx)}, device_id_type=MESH
        )
    for o in range(1, ny):
        pl.semaphore_signal(
            barrier, inc=1, device_id={"tm": lax.rem(y + o, ny) * nx + x}, device_id_type=MESH
        )

    def load(n, src, dst):
        return pltpu.make_async_copy(src, dst, in_sem.at[n])

    load(0, k_hbm, k_v).start()
    load(1, v_hbm, v_v).start()
    load(2, q_hbm, q_v).start()
    load(3, g_hbm, g_v).start()

    def order(i):
        half = lax.div(i + 1, 2)
        return jnp.where(lax.rem(i, 2) == 0, nz // 2 + half, nz // 2 - half)

    def remote(src, dst, ss, rs, where):
        return pltpu.make_async_remote_copy(
            src_ref=src, dst_ref=dst, send_sem=ss, recv_sem=rs, device_id=where, device_id_type=MESH
        )

    def pair_copy(d, j):
        return remote(
            pair_out.at[d, j], pair_in.at[d, j], pair_ss.at[d, j], pair_rs.at[d, j], {"space": partner}
        )

    def z_copy(d, j, slot):
        return remote(
            z_out.at[d, j], z_in.at[d, slot], z_ss.at[d, j], z_rs.at[d, slot], {"space": at_z(j)}
        )

    def x_copy(d, other, slot):
        return remote(
            x_out.at[d], x_in.at[d, slot], x_ss.at[d, other], x_rs.at[d, slot], {"tm": y * nx + other}
        )

    def y_copy(d, other, slot):
        return remote(
            y_out.at[d], y_in.at[d, slot], y_ss.at[d, other], y_rs.at[d, slot], {"tm": other * nx + x}
        )

    def gather_copy(d, j, head):
        return remote(
            fin.at[d, head], fin.at[d, head], ag_ss.at[d, j], fin_rs.at[d, head], {"space": at_z(j)}
        )

    def forward_copy(d, j, head):
        return remote(
            fin.at[d, head], fin.at[d, head], fw_ss.at[d, j], fin_rs.at[d, head], {"space": partner}
        )

    def give_pair(d, j, state):
        put_state(pair_out.at[d, j], *state)
        pair_copy(d, j).start()

    def keep_own(j, state):
        matrix, key_row, value_row = state
        row = lax.broadcasted_iota(jnp.int32, (16, D), 0)
        own[j, 0:D, :] = matrix
        own[j, D:STATE, :] = jnp.where(row == 0, key_row, jnp.where(row == 2, value_row, 0.0))

    def to_owner(d, off):
        j = lax.rem(z + off, nz)
        pair_copy(d, j).wait_recv()
        chip = own[j] + get_state(pair_in.at[d, j])

        @pl.when(off != 0)
        def _():
            put_packed(z_out.at[d, j], chip)
            z_copy(d, j, z).start()

        @pl.when(off == 0)
        def _():
            put_packed(z_in.at[d, z], chip)

    def scan(d):
        group = get_state(z_in.at[d, z])
        for o in range(1, nz):
            j = lax.rem(z + o, nz)
            z_copy(d, j, j).wait_recv()
            group = group + get_state(z_in.at[d, j])
        put_packed(x_out.at[d], group)
        for o in (2, 1, 3) if nx == 4 else range(1, nx):
            x_copy(d, lax.rem(x + o, nx), x).start()
        row_sum = group
        total[...] = group
        for o in range(1, nx):
            other = lax.rem(x + o, nx)
            x_copy(d, other, other).wait_recv()
            block = get_state(x_in.at[d, other])
            row_sum = row_sum + block
            before = other < x if d == 0 else other > x

            @pl.when(before)
            def _():
                total[...] += block

        put_packed(y_out.at[d], row_sum)
        for o in (2, 1, 3) if ny == 4 else range(1, ny):
            other = lax.rem(y + o, ny)

            @pl.when(other > y if d == 0 else other < y)
            def _():
                y_copy(d, other, y).start()

        for o in range(1, ny):
            other = lax.rem(y + o, ny)

            @pl.when(other < y if d == 0 else other > y)
            def _():
                y_copy(d, other, other).wait_recv()
                total[...] += get_state(y_in.at[d, other])

        put_packed(fin.at[d, space], total[...])
        forward_copy(d, z, space).start()

        def send(i, carry):
            gather_copy(d, lax.rem(z + order(i), nz), space).start()
            return carry

        lax.fori_loop(0, nz - 1, send, 0)

    def receive(d, off):
        j = lax.rem(z + off, nz)

        @pl.when(off != 0)
        def _():
            gather_copy(d, j, at_z(j)).wait_recv()
            forward_copy(d, j, at_z(j)).start()

    def receive_pair(d, off):
        j = lax.rem(z + off, nz)
        forward_copy(d, j, 2 * j + 1 - core).wait_recv()

    load(0, k_hbm, k_v).wait()
    load(1, v_hbm, v_v).wait()
    pl.semaphore_wait(barrier, 1 + (nz - 1) + (nx - 1) + (ny - 1))

    def state_of(head):
        keys, values = k_v[:, cols(head)], v_v[:, cols(head)]
        feat = jnp.maximum(keys, jnp.zeros_like(keys))
        return (
            across(feat, values),
            jnp.sum(feat.astype(F32), axis=0, keepdims=True),
            jnp.sum(values.astype(F32), axis=0, keepdims=True),
        )

    def state_step(i, carry):
        j = lax.rem(z + order(i), nz)
        give_pair(0, j, state_of(2 * j + 1 - core))
        keep_own(j, state_of(at_z(j)))

        @pl.when(i > 0)
        def _():
            to_owner(0, order(i - 1))

        return carry

    lax.fori_loop(0, nz, state_step, 0)
    to_owner(0, order(jnp.int32(nz - 1)))
    load(2, q_hbm, q_v).wait()
    load(3, g_hbm, g_v).wait()
    scan(0)

    count = ((tm + 1) * (rows * 2 * nz)).astype(F32)

    def attend(head):
        here = cols(head)
        queries, grad = q_v[:, here], g_v[:, here].astype(F32)
        feat = jnp.maximum(queries, jnp.zeros_like(queries))
        feat32 = feat.astype(F32)
        key_row, value_row = split_sums(fin[0, head, D:STATE, :].astype(F32))
        numer = times(feat, fin[0, head, 0:D, :]) + value_row
        denom = jnp.sum(feat32 * key_row, axis=1, keepdims=True) + count
        inverse = 1.0 / denom
        att_v[:, here] = (numer * inverse).astype(BF16)
        dnum = grad * inverse
        dnum_round = dnum.astype(BF16)
        dnum_v[:, here] = dnum_round
        ratio = jnp.sum(grad * numer, axis=1, keepdims=True) * (inverse * inverse)
        ratio_v[head] = ratio
        return (
            across(feat, dnum_round),
            -jnp.sum(ratio * feat32, axis=0, keepdims=True),
            jnp.sum(dnum, axis=0, keepdims=True),
        )

    def attend_step(n, carry):
        i = nz - 1 - n
        off = order(i)
        j = lax.rem(z + off, nz)
        receive(0, off)
        keep_own(j, attend(at_z(j)))
        receive_pair(0, off)
        give_pair(1, j, attend(2 * j + 1 - core))

        @pl.when(n > 0)
        def _():
            to_owner(1, order(i + 1))

        return carry

    lax.fori_loop(0, nz, attend_step, 0)
    to_owner(1, order(jnp.int32(0)))
    pltpu.make_async_copy(att_v, att_hbm, out_sem.at[0]).start()

    def query_step(head, carry):
        here = cols(head)
        key_row, _ = split_sums(fin[0, head, D:STATE, :].astype(F32))
        d_feat = times_t(dnum_v[:, here], fin[0, head, 0:D, :]) - ratio_v[head] * key_row
        gq_v[:, here] = jnp.where(q_v[:, here].astype(F32) > 0, d_feat, 0.0).astype(BF16)
        return carry

    lax.fori_loop(0, 2 * nz, query_step, 0)
    pltpu.make_async_copy(gq_v, gq_hbm, out_sem.at[1]).start()
    scan(1)

    def key_value(head):
        here = cols(head)
        keys, values = k_v[:, here], v_v[:, here]
        feat = jnp.maximum(keys, jnp.zeros_like(keys))
        matrix = fin[1, head, 0:D, :]
        key_row, value_row = split_sums(fin[1, head, D:STATE, :].astype(F32))
        gv_v[:, here] = (times(feat, matrix) + value_row).astype(BF16)
        d_key = times_t(values, matrix) + key_row
        gk_v[:, here] = jnp.where(keys.astype(F32) > 0, d_key, 0.0).astype(BF16)

    def grad_copy(j, which):
        here = pl.ds(pl.multiple_of(j * 2 * D, 2 * D), 2 * D)
        src, dst = ((gk_v, gk_hbm), (gv_v, gv_hbm))[which]
        return pltpu.make_async_copy(src.at[:, here], dst.at[:, here], grad_sem.at[which, j])

    def key_value_step(n, carry):
        off = order(nz - 1 - n)
        j = lax.rem(z + off, nz)
        receive(1, off)
        key_value(at_z(j))
        receive_pair(1, off)
        key_value(2 * j + 1 - core)
        grad_copy(j, 0).start()
        grad_copy(j, 1).start()
        return carry

    lax.fori_loop(0, nz, key_value_step, 0)

    for d in (0, 1):

        def sent(i, carry):
            off = order(i)
            j = lax.rem(z + off, nz)
            pair_copy(d, j).wait_send()
            forward_copy(d, j, at_z(j)).wait_send()

            @pl.when(off != 0)
            def _():
                z_copy(d, j, z).wait_send()
                gather_copy(d, j, space).wait_send()

            return carry

        lax.fori_loop(0, nz, sent, 0)
        for o in range(1, nx):
            x_copy(d, lax.rem(x + o, nx), x).wait_send()
        for o in range(1, ny):
            other = lax.rem(y + o, ny)

            @pl.when(other > y if d == 0 else other < y)
            def _():
                y_copy(d, other, y).wait_send()

    pltpu.make_async_copy(att_v, att_hbm, out_sem.at[0]).wait()
    pltpu.make_async_copy(gq_v, gq_hbm, out_sem.at[1]).wait()

    def stored(j, carry):
        grad_copy(j, 0).wait()
        grad_copy(j, 1).wait()
        return carry

    lax.fori_loop(0, nz, stored, 0)


def body(sizes, queries, keys, values, cotangent):
    nx, ny, nz = sizes
    heads = 2 * nz
    rows, width = queries.shape
    whole = pltpu.VMEM((rows, width), BF16)
    dma = pltpu.SemaphoreType.DMA
    like = jax.ShapeDtypeStruct((rows, width), BF16)
    return pl.pallas_call(
        functools.partial(kernel, sizes),
        out_shape=(like,) * 4,
        in_specs=[pl.BlockSpec(memory_space=pl.ANY)] * 4,
        out_specs=(pl.BlockSpec(memory_space=pl.ANY),) * 4,
        scratch_shapes=[whole] * 9
        + [
            pltpu.VMEM((heads, rows, 1), F32),
            pltpu.VMEM((nz, STATE, D), F32),
            pltpu.VMEM((2, nz, STATE, D), BF16),
            pltpu.VMEM((2, nz, STATE, D), BF16),
            pltpu.VMEM((2, nz, STATE, D), BF16),
            pltpu.VMEM((2, nz, STATE, D), BF16),
            pltpu.VMEM((2, STATE, D), BF16),
            pltpu.VMEM((2, nx, STATE, D), BF16),
            pltpu.VMEM((2, STATE, D), BF16),
            pltpu.VMEM((2, ny, STATE, D), BF16),
            pltpu.VMEM((STATE, D), F32),
            pltpu.VMEM((2, heads, STATE, D), BF16),
            dma((4,)),
            dma((2,)),
            dma((2, nz)),
            dma((2, nz)),
            dma((2, nz)),
            dma((2, nz)),
            dma((2, nz)),
            dma((2, nx)),
            dma((2, nx)),
            dma((2, ny)),
            dma((2, ny)),
            dma((2, nz)),
            dma((2, nz)),
            dma((2, heads)),
        ],
        compiler_params=pltpu.CompilerParams(collective_id=0, has_side_effects=True),
        name="scan_attention",
    )(queries, keys, values, cotangent)


def solution(mesh):
    nz = mesh.shape["space"] // 2
    nx = int(round(mesh.shape["tm"] ** 0.5))
    ny = mesh.shape["tm"] // nx
    spec = P(("tm", "space"), None)
    return jax.shard_map(
        functools.partial(body, (nx, ny, nz)),
        mesh=mesh,
        in_specs=(spec,) * 4,
        out_specs=(spec,) * 4,
        check_vma=False,
    )
```

```python
import functools

import jax
import jax.numpy as jnp
from jax import lax
from jax.experimental import pallas as pl
from jax.experimental.pallas import tpu as pltpu
from jax.sharding import PartitionSpec as P

D = 128
STATE = D + 16
MESH = pl.DeviceIdType.MESH
F32 = jnp.float32
BF16 = jnp.bfloat16


def cols(head):
    return pl.ds(pl.multiple_of(head * D, D), D)


def sums_tile(key_row, value_row):
    row = lax.broadcasted_iota(jnp.int32, (16, D), 0)
    key_low = key_row - key_row.astype(BF16).astype(F32)
    value_low = value_row - value_row.astype(BF16).astype(F32)
    tile = jnp.where(row == 0, key_row, jnp.where(row == 1, key_low, 0.0))
    tile = jnp.where(row == 2, value_row, jnp.where(row == 3, value_low, tile))
    return tile.astype(BF16)


def split_sums(tile):
    return tile[0:1] + tile[1:2], tile[2:3] + tile[3:4]


def put_state(ref, matrix, key_row, value_row):
    ref[0:D, :] = matrix.astype(BF16)
    ref[D:STATE, :] = sums_tile(key_row, value_row)


def get_state(ref):
    return ref[...].astype(F32)


def put_packed(ref, packed):
    key_row, value_row = split_sums(packed[D:STATE])
    put_state(ref, packed[0:D], key_row, value_row)


def across(left, right):
    return lax.dot_general(left, right, (((0,), (0,)), ((), ())), preferred_element_type=F32)


def times(left, right):
    return jnp.dot(left, right, preferred_element_type=F32)


def times_t(left, right):
    return lax.dot_general(left, right, (((1,), (1,)), ((), ())), preferred_element_type=F32)


def kernel(
    sizes,
    q_hbm, k_hbm, v_hbm, g_hbm,
    att_v, gq_v, k_v, v_v, fin1,
    q_v, g_v, dnum_v, ratio_v,
    own, pair_out, pair_in, z_out, z_in, x_out, x_in, y_out, y_in, total, fin0,
    in_sem,
    pair_ss, pair_rs, z_ss, z_rs, x_ss, x_rs, y_ss, y_rs, ag_ss, fw_ss, fin_rs,
):
    nx, ny, nz = sizes
    tm, space = lax.axis_index("tm"), lax.axis_index("space")
    y, x = lax.div(tm, nx), lax.rem(tm, nx)
    z, core = lax.div(space, 2), lax.rem(space, 2)
    partner = 2 * z + 1 - core
    rows = q_v.shape[0]
    fins = (fin0, fin1)

    def at_z(j):
        return 2 * j + core

    barrier = pltpu.get_barrier_semaphore()
    pl.semaphore_signal(barrier, inc=1, device_id={"space": partner}, device_id_type=MESH)
    for o in range(1, nz):
        pl.semaphore_signal(
            barrier, inc=1, device_id={"space": at_z(lax.rem(z + o, nz))}, device_id_type=MESH
        )
    for o in range(1, nx):
        pl.semaphore_signal(
            barrier, inc=1, device_id={"tm": y * nx + lax.rem(x + o, nx)}, device_id_type=MESH
        )
    for o in range(1, ny):
        pl.semaphore_signal(
            barrier, inc=1, device_id={"tm": lax.rem(y + o, ny) * nx + x}, device_id_type=MESH
        )

    def load(n, src, dst):
        return pltpu.make_async_copy(src, dst, in_sem.at[n])

    load(0, k_hbm, k_v).start()
    load(1, v_hbm, v_v).start()
    load(2, q_hbm, q_v).start()
    load(3, g_hbm, g_v).start()

    def order(i):
        half = lax.div(i + 1, 2)
        return jnp.where(lax.rem(i, 2) == 0, nz // 2 + half, nz // 2 - half)

    def remote(src, dst, ss, rs, where):
        return pltpu.make_async_remote_copy(
            src_ref=src, dst_ref=dst, send_sem=ss, recv_sem=rs, device_id=where, device_id_type=MESH
        )

    def pair_copy(d, j):
        return remote(
            pair_out.at[d, j], pair_in.at[d, j], pair_ss.at[d, j], pair_rs.at[d, j], {"space": partner}
        )

    def z_copy(d, j, slot):
        return remote(
            z_out.at[d, j], z_in.at[d, slot], z_ss.at[d, j], z_rs.at[d, slot], {"space": at_z(j)}
        )

    def x_copy(d, other, slot):
        return remote(
            x_out.at[d], x_in.at[d, slot], x_ss.at[d, other], x_rs.at[d, slot], {"tm": y * nx + other}
        )

    def y_copy(d, other, slot):
        return remote(
            y_out.at[d], y_in.at[d, slot], y_ss.at[d, other], y_rs.at[d, slot], {"tm": other * nx + x}
        )

    def gather_copy(d, j, head):
        return remote(
            fins[d].at[head], fins[d].at[head], ag_ss.at[d, j], fin_rs.at[d, head], {"space": at_z(j)}
        )

    def forward_copy(d, j, head):
        return remote(
            fins[d].at[head], fins[d].at[head], fw_ss.at[d, j], fin_rs.at[d, head], {"space": partner}
        )

    def give_pair(d, j, state):
        put_state(pair_out.at[d, j], *state)
        pair_copy(d, j).start()

    def keep_own(j, state):
        matrix, key_row, value_row = state
        row = lax.broadcasted_iota(jnp.int32, (16, D), 0)
        own[j, 0:D, :] = matrix
        own[j, D:STATE, :] = jnp.where(row == 0, key_row, jnp.where(row == 2, value_row, 0.0))

    def to_owner(d, off):
        j = lax.rem(z + off, nz)
        pair_copy(d, j).wait_recv()
        chip = own[j] + get_state(pair_in.at[d, j])

        @pl.when(off != 0)
        def _():
            put_packed(z_out.at[d, j], chip)
            z_copy(d, j, z).start()

        @pl.when(off == 0)
        def _():
            put_packed(z_in.at[d, z], chip)

    def sum_z(d):
        group = get_state(z_in.at[d, z])
        for o in range(1, nz):
            j = lax.rem(z + o, nz)
            z_copy(d, j, j).wait_recv()
            group = group + get_state(z_in.at[d, j])
        total[...] = group

    def scan_x(d):
        group = total[...]
        put_packed(x_out.at[d], group)
        for o in (2, 1, 3) if nx == 4 else range(1, nx):
            x_copy(d, lax.rem(x + o, nx), x).start()
        row_sum = group
        for o in range(1, nx):
            other = lax.rem(x + o, nx)
            x_copy(d, other, other).wait_recv()
            block = get_state(x_in.at[d, other])
            row_sum = row_sum + block
            before = other < x if d == 0 else other > x

            @pl.when(before)
            def _():
                total[...] += block

        put_packed(y_out.at[d], row_sum)

    def scan_y(d):
        for o in (2, 1, 3) if ny == 4 else range(1, ny):
            other = lax.rem(y + o, ny)

            @pl.when(other > y if d == 0 else other < y)
            def _():
                y_copy(d, other, y).start()

        for o in range(1, ny):
            other = lax.rem(y + o, ny)

            @pl.when(other < y if d == 0 else other > y)
            def _():
                y_copy(d, other, other).wait_recv()
                total[...] += get_state(y_in.at[d, other])

    def spread(d):
        put_packed(fins[d].at[space], total[...])
        forward_copy(d, z, space).start()

        def send(i, carry):
            gather_copy(d, lax.rem(z + order(i), nz), space).start()
            return carry

        lax.fori_loop(0, nz - 1, send, 0)

    def receive(d, off):
        j = lax.rem(z + off, nz)

        @pl.when(off != 0)
        def _():
            gather_copy(d, j, at_z(j)).wait_recv()
            forward_copy(d, j, at_z(j)).start()

    def receive_pair(d, off):
        j = lax.rem(z + off, nz)
        forward_copy(d, j, 2 * j + 1 - core).wait_recv()

    load(0, k_hbm, k_v).wait()
    load(1, v_hbm, v_v).wait()
    pl.semaphore_wait(barrier, 1 + (nz - 1) + (nx - 1) + (ny - 1))

    def state_of(head):
        keys, values = k_v[:, cols(head)], v_v[:, cols(head)]
        feat = jnp.maximum(keys, jnp.zeros_like(keys))
        return (
            across(feat, values),
            jnp.sum(feat.astype(F32), axis=0, keepdims=True),
            jnp.sum(values.astype(F32), axis=0, keepdims=True),
        )

    def state_step(i, carry):
        j = lax.rem(z + order(i), nz)
        give_pair(0, j, state_of(2 * j + 1 - core))
        keep_own(j, state_of(at_z(j)))

        @pl.when(i > 0)
        def _():
            to_owner(0, order(i - 1))

        return carry

    lax.fori_loop(0, nz, state_step, 0)
    to_owner(0, order(jnp.int32(nz - 1)))
    load(2, q_hbm, q_v).wait()
    load(3, g_hbm, g_v).wait()
    sum_z(0)
    scan_x(0)
    scan_y(0)
    spread(0)

    count = ((tm + 1) * (rows * 2 * nz)).astype(F32)

    def attend(head):
        here = cols(head)
        queries, grad = q_v[:, here], g_v[:, here].astype(F32)
        feat = jnp.maximum(queries, jnp.zeros_like(queries))
        feat32 = feat.astype(F32)
        key_row, value_row = split_sums(fin0[head, D:STATE, :].astype(F32))
        numer = times(feat, fin0[head, 0:D, :]) + value_row
        denom = jnp.sum(feat32 * key_row, axis=1, keepdims=True) + count
        inverse = 1.0 / denom
        att_v[:, here] = (numer * inverse).astype(BF16)
        dnum = grad * inverse
        dnum_round = dnum.astype(BF16)
        dnum_v[:, here] = dnum_round
        ratio = jnp.sum(grad * numer, axis=1, keepdims=True) * (inverse * inverse)
        ratio_v[head] = ratio
        return (
            across(feat, dnum_round),
            -jnp.sum(ratio * feat32, axis=0, keepdims=True),
            jnp.sum(dnum, axis=0, keepdims=True),
        )

    def attend_step(n, carry):
        i = nz - 1 - n
        off = order(i)
        j = lax.rem(z + off, nz)
        receive(0, off)
        keep_own(j, attend(at_z(j)))
        receive_pair(0, off)
        give_pair(1, j, attend(2 * j + 1 - core))

        @pl.when(n > 0)
        def _():
            to_owner(1, order(i + 1))

        return carry

    lax.fori_loop(0, nz, attend_step, 0)
    to_owner(1, order(jnp.int32(0)))

    def query_step(head, carry):
        here = cols(head)
        key_row, _ = split_sums(fin0[head, D:STATE, :].astype(F32))
        d_feat = times_t(dnum_v[:, here], fin0[head, 0:D, :]) - ratio_v[head] * key_row
        gq_v[:, here] = jnp.where(q_v[:, here].astype(F32) > 0, d_feat, 0.0).astype(BF16)
        return carry

    lax.fori_loop(0, 2 * nz, query_step, 0)
    sum_z(1)
    scan_x(1)
    scan_y(1)
    spread(1)

    def receive_step(n, carry):
        off = order(nz - 1 - n)
        receive(1, off)
        receive_pair(1, off)
        return carry

    lax.fori_loop(0, nz, receive_step, 0)

    for d in (0, 1):

        def sent(i, carry):
            off = order(i)
            j = lax.rem(z + off, nz)
            pair_copy(d, j).wait_send()
            forward_copy(d, j, at_z(j)).wait_send()

            @pl.when(off != 0)
            def _():
                z_copy(d, j, z).wait_send()
                gather_copy(d, j, space).wait_send()

            return carry

        lax.fori_loop(0, nz, sent, 0)
        for o in range(1, nx):
            x_copy(d, lax.rem(x + o, nx), x).wait_send()
        for o in range(1, ny):
            other = lax.rem(y + o, ny)

            @pl.when(other > y if d == 0 else other < y)
            def _():
                y_copy(d, other, y).wait_send()


def finish_kernel(att_v, gq_v, k_v, v_v, fin1, att_hbm, gq_hbm, gk_hbm, gv_hbm, gk_v, gv_v, sem, grad_sem):
    att_copy = pltpu.make_async_copy(att_v, att_hbm, sem.at[0])
    gq_copy = pltpu.make_async_copy(gq_v, gq_hbm, sem.at[1])
    att_copy.start()
    gq_copy.start()
    pairs = fin1.shape[0] // 2

    def key_value(head):
        here = cols(head)
        keys, values = k_v[:, here], v_v[:, here]
        feat = jnp.maximum(keys, jnp.zeros_like(keys))
        matrix = fin1[head, 0:D, :]
        key_row, value_row = split_sums(fin1[head, D:STATE, :].astype(F32))
        gv_v[:, here] = (times(feat, matrix) + value_row).astype(BF16)
        d_key = times_t(values, matrix) + key_row
        gk_v[:, here] = jnp.where(keys.astype(F32) > 0, d_key, 0.0).astype(BF16)

    def grad_copy(j, which):
        here = pl.ds(pl.multiple_of(j * 2 * D, 2 * D), 2 * D)
        src, dst = ((gk_v, gk_hbm), (gv_v, gv_hbm))[which]
        return pltpu.make_async_copy(src.at[:, here], dst.at[:, here], grad_sem.at[which, j])

    def step(j, carry):
        key_value(2 * j)
        key_value(2 * j + 1)
        grad_copy(j, 0).start()
        grad_copy(j, 1).start()
        return carry

    lax.fori_loop(0, pairs, step, 0)
    att_copy.wait()
    gq_copy.wait()

    def stored(j, carry):
        grad_copy(j, 0).wait()
        grad_copy(j, 1).wait()
        return carry

    lax.fori_loop(0, pairs, stored, 0)


def body(sizes, queries, keys, values, cotangent):
    nx, ny, nz = sizes
    heads = 2 * nz
    rows, width = queries.shape
    whole = pltpu.VMEM((rows, width), BF16)
    dma = pltpu.SemaphoreType.DMA
    like = jax.ShapeDtypeStruct((rows, width), BF16)
    in_vmem = pl.BlockSpec(memory_space=pltpu.VMEM)
    in_hbm = pl.BlockSpec(memory_space=pl.ANY)
    held = pl.pallas_call(
        functools.partial(kernel, sizes),
        out_shape=(whole,) * 4 + (pltpu.VMEM((heads, STATE, D), BF16),),
        in_specs=[pl.BlockSpec(memory_space=pltpu.HBM)] * 4,
        out_specs=(in_vmem,) * 5,
        scratch_shapes=[whole] * 3
        + [
            pltpu.VMEM((heads, rows, 1), F32),
            pltpu.VMEM((nz, STATE, D), F32),
            pltpu.VMEM((2, nz, STATE, D), BF16),
            pltpu.VMEM((2, nz, STATE, D), BF16),
            pltpu.VMEM((2, nz, STATE, D), BF16),
            pltpu.VMEM((2, nz, STATE, D), BF16),
            pltpu.VMEM((2, STATE, D), BF16),
            pltpu.VMEM((2, nx, STATE, D), BF16),
            pltpu.VMEM((2, STATE, D), BF16),
            pltpu.VMEM((2, ny, STATE, D), BF16),
            pltpu.VMEM((STATE, D), F32),
            pltpu.VMEM((heads, STATE, D), BF16),
            dma((4,)),
            dma((2, nz)),
            dma((2, nz)),
            dma((2, nz)),
            dma((2, nz)),
            dma((2, nx)),
            dma((2, nx)),
            dma((2, ny)),
            dma((2, ny)),
            dma((2, nz)),
            dma((2, nz)),
            dma((2, heads)),
        ],
        compiler_params=pltpu.CompilerParams(
            collective_id=0, has_side_effects=True, vmem_limit_bytes=32 << 20
        ),
        name="scan_attention",
    )(*(pltpu.with_memory_space_constraint(a, pltpu.HBM) for a in (queries, keys, values, cotangent)))
    return pl.pallas_call(
        finish_kernel,
        out_shape=(like,) * 4,
        in_specs=[in_vmem] * 5,
        out_specs=(in_hbm,) * 4,
        scratch_shapes=[whole] * 2 + [dma((2,)), dma((2, nz))],
        compiler_params=pltpu.CompilerParams(vmem_limit_bytes=16 << 20),
        name="finish",
    )(*held)


def solution(mesh):
    nz = mesh.shape["space"] // 2
    nx = int(round(mesh.shape["tm"] ** 0.5))
    ny = mesh.shape["tm"] // nx
    spec = P(("tm", "space"), None)
    return jax.shard_map(
        functools.partial(body, (nx, ny, nz)),
        mesh=mesh,
        in_specs=(spec,) * 4,
        out_specs=(spec,) * 4,
        check_vma=False,
    )
```

```python
import functools

import jax
import jax.numpy as jnp
from jax import lax
from jax.experimental import pallas as pl
from jax.experimental.pallas import tpu as pltpu
from jax.sharding import PartitionSpec as P

D = 128
STATE = D + 16
MESH = pl.DeviceIdType.MESH
F32 = jnp.float32
BF16 = jnp.bfloat16


def cols(head):
    return pl.ds(pl.multiple_of(head * D, D), D)


def sums_tile(key_row, value_row):
    row = lax.broadcasted_iota(jnp.int32, (16, D), 0)
    key_low = key_row - key_row.astype(BF16).astype(F32)
    value_low = value_row - value_row.astype(BF16).astype(F32)
    tile = jnp.where(row == 0, key_row, jnp.where(row == 1, key_low, 0.0))
    tile = jnp.where(row == 2, value_row, jnp.where(row == 3, value_low, tile))
    return tile.astype(BF16)


def split_sums(tile):
    return tile[0:1] + tile[1:2], tile[2:3] + tile[3:4]


def put_state(ref, matrix, key_row, value_row):
    ref[0:D, :] = matrix.astype(BF16)
    ref[D:STATE, :] = sums_tile(key_row, value_row)


def get_state(ref):
    return ref[...].astype(F32)


def put_packed(ref, packed):
    key_row, value_row = split_sums(packed[D:STATE])
    put_state(ref, packed[0:D], key_row, value_row)


def across(left, right):
    return lax.dot_general(left, right, (((0,), (0,)), ((), ())), preferred_element_type=F32)


def times(left, right):
    return jnp.dot(left, right, preferred_element_type=F32)


def times_t(left, right):
    return lax.dot_general(left, right, (((1,), (1,)), ((), ())), preferred_element_type=F32)


def kernel(
    sizes,
    q_hbm, k_hbm, v_hbm, g_hbm,
    att_v, gq_v, gk_v, gv_v,
    q_v, k_v, v_v, g_v, dnum_v, ratio_v,
    own, pair_out, pair_in, z_out, z_in, x_out, x_in, y_out, y_in, total, fin0, fin1,
    in_sem,
    pair_ss, pair_rs, z_ss, z_rs, x_ss, x_rs, y_ss, y_rs, ag_ss, fw_ss, fin_rs,
):
    nx, ny, nz = sizes
    tm, space = lax.axis_index("tm"), lax.axis_index("space")
    y, x = lax.div(tm, nx), lax.rem(tm, nx)
    z, core = lax.div(space, 2), lax.rem(space, 2)
    partner = 2 * z + 1 - core
    rows = q_v.shape[0]
    fins = (fin0, fin1)

    def at_z(j):
        return 2 * j + core

    barrier = pltpu.get_barrier_semaphore()
    pl.semaphore_signal(barrier, inc=1, device_id={"space": partner}, device_id_type=MESH)
    for o in range(1, nz):
        pl.semaphore_signal(
            barrier, inc=1, device_id={"space": at_z(lax.rem(z + o, nz))}, device_id_type=MESH
        )
    for o in range(1, nx):
        pl.semaphore_signal(
            barrier, inc=1, device_id={"tm": y * nx + lax.rem(x + o, nx)}, device_id_type=MESH
        )
    for o in range(1, ny):
        pl.semaphore_signal(
            barrier, inc=1, device_id={"tm": lax.rem(y + o, ny) * nx + x}, device_id_type=MESH
        )

    def load(n, src, dst):
        return pltpu.make_async_copy(src, dst, in_sem.at[n])

    load(0, k_hbm, k_v).start()
    load(1, v_hbm, v_v).start()
    load(2, q_hbm, q_v).start()
    load(3, g_hbm, g_v).start()

    def order(i):
        half = lax.div(i + 1, 2)
        return jnp.where(lax.rem(i, 2) == 0, nz // 2 + half, nz // 2 - half)

    def remote(src, dst, ss, rs, where):
        return pltpu.make_async_remote_copy(
            src_ref=src, dst_ref=dst, send_sem=ss, recv_sem=rs, device_id=where, device_id_type=MESH
        )

    def pair_copy(d, j):
        return remote(
            pair_out.at[d, j], pair_in.at[d, j], pair_ss.at[d, j], pair_rs.at[d, j], {"space": partner}
        )

    def z_copy(d, j, slot):
        return remote(
            z_out.at[d, j], z_in.at[d, slot], z_ss.at[d, j], z_rs.at[d, slot], {"space": at_z(j)}
        )

    def x_copy(d, other, slot):
        return remote(
            x_out.at[d], x_in.at[d, slot], x_ss.at[d, other], x_rs.at[d, slot], {"tm": y * nx + other}
        )

    def y_copy(d, other, slot):
        return remote(
            y_out.at[d], y_in.at[d, slot], y_ss.at[d, other], y_rs.at[d, slot], {"tm": other * nx + x}
        )

    def gather_copy(d, j, head):
        return remote(
            fins[d].at[head], fins[d].at[head], ag_ss.at[d, j], fin_rs.at[d, head], {"space": at_z(j)}
        )

    def forward_copy(d, j, head):
        return remote(
            fins[d].at[head], fins[d].at[head], fw_ss.at[d, j], fin_rs.at[d, head], {"space": partner}
        )

    def give_pair(d, j, state):
        put_state(pair_out.at[d, j], *state)
        pair_copy(d, j).start()

    def keep_own(j, state):
        matrix, key_row, value_row = state
        row = lax.broadcasted_iota(jnp.int32, (16, D), 0)
        own[j, 0:D, :] = matrix
        own[j, D:STATE, :] = jnp.where(row == 0, key_row, jnp.where(row == 2, value_row, 0.0))

    def to_owner(d, off):
        j = lax.rem(z + off, nz)
        pair_copy(d, j).wait_recv()
        chip = own[j] + get_state(pair_in.at[d, j])

        @pl.when(off != 0)
        def _():
            put_packed(z_out.at[d, j], chip)
            z_copy(d, j, z).start()

        @pl.when(off == 0)
        def _():
            put_packed(z_in.at[d, z], chip)

    def sum_z(d):
        group = get_state(z_in.at[d, z])
        for o in range(1, nz):
            j = lax.rem(z + o, nz)
            z_copy(d, j, j).wait_recv()
            group = group + get_state(z_in.at[d, j])
        total[...] = group

    def scan_x(d):
        group = total[...]
        put_packed(x_out.at[d], group)
        for o in (2, 1, 3) if nx == 4 else range(1, nx):
            x_copy(d, lax.rem(x + o, nx), x).start()
        row_sum = group
        for o in range(1, nx):
            other = lax.rem(x + o, nx)
            x_copy(d, other, other).wait_recv()
            block = get_state(x_in.at[d, other])
            row_sum = row_sum + block
            before = other < x if d == 0 else other > x

            @pl.when(before)
            def _():
                total[...] += block

        put_packed(y_out.at[d], row_sum)

    def scan_y(d):
        for o in (2, 1, 3) if ny == 4 else range(1, ny):
            other = lax.rem(y + o, ny)

            @pl.when(other > y if d == 0 else other < y)
            def _():
                y_copy(d, other, y).start()

        for o in range(1, ny):
            other = lax.rem(y + o, ny)

            @pl.when(other < y if d == 0 else other > y)
            def _():
                y_copy(d, other, other).wait_recv()
                total[...] += get_state(y_in.at[d, other])

    def spread(d):
        put_packed(fins[d].at[space], total[...])
        forward_copy(d, z, space).start()

        def send(i, carry):
            gather_copy(d, lax.rem(z + order(i), nz), space).start()
            return carry

        lax.fori_loop(0, nz - 1, send, 0)

    def receive(d, off):
        j = lax.rem(z + off, nz)

        @pl.when(off != 0)
        def _():
            gather_copy(d, j, at_z(j)).wait_recv()
            forward_copy(d, j, at_z(j)).start()

    def receive_pair(d, off):
        j = lax.rem(z + off, nz)
        forward_copy(d, j, 2 * j + 1 - core).wait_recv()

    load(0, k_hbm, k_v).wait()
    load(1, v_hbm, v_v).wait()

    def state_of(head):
        keys, values = k_v[:, cols(head)], v_v[:, cols(head)]
        feat = jnp.maximum(keys, jnp.zeros_like(keys))
        return (
            across(feat, values),
            jnp.sum(feat.astype(F32), axis=0, keepdims=True),
            jnp.sum(values.astype(F32), axis=0, keepdims=True),
        )

    def pair_step(j, carry):
        put_state(pair_out.at[0, j], *state_of(2 * j + 1 - core))
        return carry

    lax.fori_loop(0, nz, pair_step, 0)
    pl.semaphore_wait(barrier, 1 + (nz - 1) + (nx - 1) + (ny - 1))

    def pair_send(i, carry):
        pair_copy(0, lax.rem(z + order(i), nz)).start()
        return carry

    lax.fori_loop(0, nz, pair_send, 0)

    def own_step(i, carry):
        off = order(i)
        j = lax.rem(z + off, nz)
        keep_own(j, state_of(at_z(j)))
        to_owner(0, off)
        return carry

    lax.fori_loop(0, nz, own_step, 0)
    load(2, q_hbm, q_v).wait()
    load(3, g_hbm, g_v).wait()
    sum_z(0)
    scan_x(0)
    scan_y(0)
    spread(0)

    count = ((tm + 1) * (rows * 2 * nz)).astype(F32)

    def attend(head):
        here = cols(head)
        queries, grad = q_v[:, here], g_v[:, here].astype(F32)
        feat = jnp.maximum(queries, jnp.zeros_like(queries))
        feat32 = feat.astype(F32)
        key_row, value_row = split_sums(fin0[head, D:STATE, :].astype(F32))
        numer = times(feat, fin0[head, 0:D, :]) + value_row
        denom = jnp.sum(feat32 * key_row, axis=1, keepdims=True) + count
        inverse = 1.0 / denom
        att_v[:, here] = (numer * inverse).astype(BF16)
        dnum = grad * inverse
        dnum_round = dnum.astype(BF16)
        dnum_v[:, here] = dnum_round
        ratio = jnp.sum(grad * numer, axis=1, keepdims=True) * (inverse * inverse)
        ratio_v[head] = ratio
        return (
            across(feat, dnum_round),
            -jnp.sum(ratio * feat32, axis=0, keepdims=True),
            jnp.sum(dnum, axis=0, keepdims=True),
        )

    def attend_own(n):
        off = order(nz - 1 - n)
        receive(0, off)
        j = lax.rem(z + off, nz)
        keep_own(j, attend(at_z(j)))

    def attend_pair(n):
        off = order(nz - 1 - n)
        receive_pair(0, off)
        j = lax.rem(z + off, nz)
        give_pair(1, j, attend(2 * j + 1 - core))

    attend_own(jnp.int32(0))

    def attend_step(n, carry):
        attend_own(n)
        attend_pair(n - 1)

        @pl.when(n > 1)
        def _():
            to_owner(1, order(nz + 1 - n))

        return carry

    lax.fori_loop(1, nz, attend_step, 0)
    attend_pair(jnp.int32(nz - 1))
    to_owner(1, order(jnp.int32(1)))
    to_owner(1, order(jnp.int32(0)))

    def query_step(head, carry):
        here = cols(head)
        key_row, _ = split_sums(fin0[head, D:STATE, :].astype(F32))
        d_feat = times_t(dnum_v[:, here], fin0[head, 0:D, :]) - ratio_v[head] * key_row
        gq_v[:, here] = jnp.where(q_v[:, here].astype(F32) > 0, d_feat, 0.0).astype(BF16)
        return carry

    lax.fori_loop(0, 2 * nz, query_step, 0)
    sum_z(1)
    scan_x(1)
    scan_y(1)
    spread(1)

    def key_value(head):
        here = cols(head)
        keys, values = k_v[:, here], v_v[:, here]
        feat = jnp.maximum(keys, jnp.zeros_like(keys))
        matrix = fin1[head, 0:D, :]
        key_row, value_row = split_sums(fin1[head, D:STATE, :].astype(F32))
        gv_v[:, here] = (times(feat, matrix) + value_row).astype(BF16)
        d_key = times_t(values, matrix) + key_row
        gk_v[:, here] = jnp.where(keys.astype(F32) > 0, d_key, 0.0).astype(BF16)

    def grads_own(n):
        off = order(nz - 1 - n)
        receive(1, off)
        key_value(at_z(lax.rem(z + off, nz)))

    def grads_pair(n):
        off = order(nz - 1 - n)
        receive_pair(1, off)
        key_value(2 * lax.rem(z + off, nz) + 1 - core)

    grads_own(jnp.int32(0))

    def grads_step(n, carry):
        grads_own(n)
        grads_pair(n - 1)
        return carry

    lax.fori_loop(1, nz, grads_step, 0)
    grads_pair(jnp.int32(nz - 1))

    for d in (0, 1):

        def sent(i, carry):
            off = order(i)
            j = lax.rem(z + off, nz)
            pair_copy(d, j).wait_send()
            forward_copy(d, j, at_z(j)).wait_send()

            @pl.when(off != 0)
            def _():
                z_copy(d, j, z).wait_send()
                gather_copy(d, j, space).wait_send()

            return carry

        lax.fori_loop(0, nz, sent, 0)
        for o in range(1, nx):
            x_copy(d, lax.rem(x + o, nx), x).wait_send()
        for o in range(1, ny):
            other = lax.rem(y + o, ny)

            @pl.when(other > y if d == 0 else other < y)
            def _():
                y_copy(d, other, y).wait_send()


def store_kernel(*refs):
    count = (len(refs) - 1) // 2
    sources, targets, sem = refs[:count], refs[count : 2 * count], refs[-1]
    half = sources[0].shape[0] // 2
    copies = [
        pltpu.make_async_copy(src.at[pl.ds(part * half, half)], dst.at[pl.ds(part * half, half)], sem.at[n, part])
        for n, (src, dst) in enumerate(zip(sources, targets))
        for part in range(2)
    ]
    for copy in copies:
        copy.start()
    for copy in copies:
        copy.wait()


def body(sizes, queries, keys, values, cotangent):
    nx, ny, nz = sizes
    heads = 2 * nz
    rows, width = queries.shape
    whole = pltpu.VMEM((rows, width), BF16)
    dma = pltpu.SemaphoreType.DMA
    like = jax.ShapeDtypeStruct((rows, width), BF16)
    in_vmem = pl.BlockSpec(memory_space=pltpu.VMEM)
    in_hbm = pl.BlockSpec(memory_space=pl.ANY)
    held = pl.pallas_call(
        functools.partial(kernel, sizes),
        out_shape=(whole,) * 4,
        in_specs=[pl.BlockSpec(memory_space=pltpu.HBM)] * 4,
        out_specs=(in_vmem,) * 4,
        scratch_shapes=[whole] * 5
        + [
            pltpu.VMEM((heads, rows, 1), F32),
            pltpu.VMEM((nz, STATE, D), F32),
            pltpu.VMEM((2, nz, STATE, D), BF16),
            pltpu.VMEM((2, nz, STATE, D), BF16),
            pltpu.VMEM((2, nz, STATE, D), BF16),
            pltpu.VMEM((2, nz, STATE, D), BF16),
            pltpu.VMEM((2, STATE, D), BF16),
            pltpu.VMEM((2, nx, STATE, D), BF16),
            pltpu.VMEM((2, STATE, D), BF16),
            pltpu.VMEM((2, ny, STATE, D), BF16),
            pltpu.VMEM((STATE, D), F32),
            pltpu.VMEM((heads, STATE, D), BF16),
            pltpu.VMEM((heads, STATE, D), BF16),
            dma((4,)),
            dma((2, nz)),
            dma((2, nz)),
            dma((2, nz)),
            dma((2, nz)),
            dma((2, nx)),
            dma((2, nx)),
            dma((2, ny)),
            dma((2, ny)),
            dma((2, nz)),
            dma((2, nz)),
            dma((2, heads)),
        ],
        compiler_params=pltpu.CompilerParams(
            collective_id=0, has_side_effects=True, vmem_limit_bytes=32 << 20
        ),
        name="scan_attention",
    )(*(pltpu.with_memory_space_constraint(a, pltpu.HBM) for a in (queries, keys, values, cotangent)))
    return pl.pallas_call(
        store_kernel,
        out_shape=(like,) * 4,
        in_specs=[in_vmem] * 4,
        out_specs=(in_hbm,) * 4,
        scratch_shapes=[dma((4, 2))],
        compiler_params=pltpu.CompilerParams(vmem_limit_bytes=16 << 20),
        name="store",
    )(*held)


def solution(mesh):
    nz = mesh.shape["space"] // 2
    nx = int(round(mesh.shape["tm"] ** 0.5))
    ny = mesh.shape["tm"] // nx
    spec = P(("tm", "space"), None)
    return jax.shard_map(
        functools.partial(body, (nx, ny, nz)),
        mesh=mesh,
        in_specs=(spec,) * 4,
        out_specs=(spec,) * 4,
        check_vma=False,
    )
```

```python
import functools

import jax
import jax.numpy as jnp
from jax import lax
from jax.experimental import pallas as pl
from jax.experimental.pallas import tpu as pltpu
from jax.sharding import PartitionSpec as P

D = 128
STATE = D + 16
PARTS = ((0, 64), (64, STATE - 64))
LAG = 3
MESH = pl.DeviceIdType.MESH
F32 = jnp.float32
BF16 = jnp.bfloat16


def cols(head):
    return pl.ds(pl.multiple_of(head * D, D), D)


def sums_tile(key_row, value_row):
    row = lax.broadcasted_iota(jnp.int32, (16, D), 0)
    key_low = key_row - key_row.astype(BF16).astype(F32)
    value_low = value_row - value_row.astype(BF16).astype(F32)
    tile = jnp.where(row == 0, key_row, jnp.where(row == 1, key_low, 0.0))
    tile = jnp.where(row == 2, value_row, jnp.where(row == 3, value_low, tile))
    return tile.astype(BF16)


def split_sums(tile):
    return tile[0:1] + tile[1:2], tile[2:3] + tile[3:4]


def put_state(ref, matrix, key_row, value_row):
    ref[0:D, :] = matrix.astype(BF16)
    ref[D:STATE, :] = sums_tile(key_row, value_row)


def put_packed(ref, packed):
    for part, (start, size) in enumerate(PARTS):
        put_part(ref, part, packed[start : start + size])


def put_part(ref, part, packed):
    start, size = PARTS[part]
    stop = min(start + size, D)
    ref[start:stop, :] = packed[: stop - start].astype(BF16)
    if start + size > D:
        ref[D:STATE, :] = sums_tile(*split_sums(packed[stop - start :]))


def get_part(ref, part):
    start, size = PARTS[part]
    return ref[start : start + size, :].astype(F32)


def across(left, right):
    return lax.dot_general(left, right, (((0,), (0,)), ((), ())), preferred_element_type=F32)


def times(left, right):
    return jnp.dot(left, right, preferred_element_type=F32)


def times_t(left, right):
    return lax.dot_general(left, right, (((1,), (1,)), ((), ())), preferred_element_type=F32)


def kernel(
    sizes,
    q_hbm, k_hbm, v_hbm, g_hbm,
    att_v, gq_v, gk_v, gv_v,
    q_v, k_v, v_v, g_v, dnum_v, ratio_v,
    own, pair_out, pair_in, z_out, z_in, x_out, x_in, y_out, y_in, total, fin0, fin1,
    in_sem,
    pair_ss, pair_rs, z_ss, z_rs, x_ss, x_rs, y_ss, y_rs, ag_ss, ag_rs, fw_ss, fw_rs,
):
    nx, ny, nz = sizes
    tm, space = lax.axis_index("tm"), lax.axis_index("space")
    y, x = lax.div(tm, nx), lax.rem(tm, nx)
    z, core = lax.div(space, 2), lax.rem(space, 2)
    partner = 2 * z + 1 - core
    rows = q_v.shape[0]
    fins = (fin0, fin1)

    def at_z(j):
        return 2 * j + core

    barrier = pltpu.get_barrier_semaphore()
    pl.semaphore_signal(barrier, inc=1, device_id={"space": partner}, device_id_type=MESH)
    for o in range(1, nz):
        pl.semaphore_signal(
            barrier, inc=1, device_id={"space": at_z(lax.rem(z + o, nz))}, device_id_type=MESH
        )
    for o in range(1, nx):
        pl.semaphore_signal(
            barrier, inc=1, device_id={"tm": y * nx + lax.rem(x + o, nx)}, device_id_type=MESH
        )
    for o in range(1, ny):
        pl.semaphore_signal(
            barrier, inc=1, device_id={"tm": lax.rem(y + o, ny) * nx + x}, device_id_type=MESH
        )

    def load(n, src, dst):
        return pltpu.make_async_copy(src, dst, in_sem.at[n])

    load(0, k_hbm, k_v).start()
    load(1, v_hbm, v_v).start()
    load(2, q_hbm, q_v).start()
    load(3, g_hbm, g_v).start()

    def order(i):
        half = lax.div(i + 1, 2)
        return jnp.where(lax.rem(i, 2) == 0, nz // 2 + half, nz // 2 - half)

    def remote(src, dst, ss, rs, where):
        return pltpu.make_async_remote_copy(
            src_ref=src, dst_ref=dst, send_sem=ss, recv_sem=rs, device_id=where, device_id_type=MESH
        )

    def pair_copy(d, j):
        return remote(
            pair_out.at[d, j], pair_in.at[d, j], pair_ss.at[d, j], pair_rs.at[d, j], {"space": partner}
        )

    def z_copy(d, part, j, slot):
        rows_of = pl.ds(*PARTS[part])
        return remote(
            z_out.at[d, j, rows_of], z_in.at[d, slot, rows_of],
            z_ss.at[d, part, j], z_rs.at[d, part, slot], {"space": at_z(j)},
        )

    def x_copy(d, part, other, slot):
        rows_of = pl.ds(*PARTS[part])
        return remote(
            x_out.at[d, rows_of], x_in.at[d, slot, rows_of],
            x_ss.at[d, part, other], x_rs.at[d, part, slot], {"tm": y * nx + other},
        )

    def y_copy(d, part, other, slot):
        rows_of = pl.ds(*PARTS[part])
        return remote(
            y_out.at[d, rows_of], y_in.at[d, slot, rows_of],
            y_ss.at[d, part, other], y_rs.at[d, part, slot], {"tm": other * nx + x},
        )

    def gather_copy(d, part, j, head):
        here = fins[d].at[head, pl.ds(*PARTS[part])]
        return remote(here, here, ag_ss.at[d, part, j], ag_rs.at[d, part, head], {"space": at_z(j)})

    def forward_copy(d, j, head):
        here = fins[d].at[head]
        return remote(here, here, fw_ss.at[d, j], fw_rs.at[d, head], {"space": partner})

    def give_pair(d, j, state):
        put_state(pair_out.at[d, j], *state)
        pair_copy(d, j).start()

    def keep_own(j, state):
        matrix, key_row, value_row = state
        row = lax.broadcasted_iota(jnp.int32, (16, D), 0)
        own[j, 0:D, :] = matrix
        own[j, D:STATE, :] = jnp.where(row == 0, key_row, jnp.where(row == 2, value_row, 0.0))

    def to_owner(d, off, parts):
        j = lax.rem(z + off, nz)
        pair_copy(d, j).wait_recv()
        chip = own[j] + pair_in[d, j].astype(F32)

        @pl.when(off != 0)
        def _():
            put_packed(z_out.at[d, j], chip)
            for part in range(parts):
                z_copy(d, part, j, z).start()

        @pl.when(off == 0)
        def _():
            put_packed(z_in.at[d, z], chip)

    def sum_z(d, part):
        start, size = PARTS[part]
        group = get_part(z_in.at[d, z], part)
        for o in range(1, nz):
            j = lax.rem(z + o, nz)
            z_copy(d, part, j, j).wait_recv()
            group = group + get_part(z_in.at[d, j], part)
        put_part(x_out.at[d], part, group)
        for o in (2, 1, 3) if nx == 4 else range(1, nx):
            x_copy(d, part, lax.rem(x + o, nx), x).start()
        total[start : start + size, :] = group

    def scan_x(d, part):
        start, size = PARTS[part]
        row_sum = total[start : start + size, :]
        for o in range(1, nx):
            other = lax.rem(x + o, nx)
            x_copy(d, part, other, other).wait_recv()
            block = get_part(x_in.at[d, other], part)
            row_sum = row_sum + block

            @pl.when(other < x if d == 0 else other > x)
            def _():
                total[start : start + size, :] += block

        put_part(y_out.at[d], part, row_sum)
        for o in (2, 1, 3) if ny == 4 else range(1, ny):
            other = lax.rem(y + o, ny)

            @pl.when(other > y if d == 0 else other < y)
            def _():
                y_copy(d, part, other, y).start()

    def scan_y(d, part):
        start, size = PARTS[part]
        for o in range(1, ny):
            other = lax.rem(y + o, ny)

            @pl.when(other < y if d == 0 else other > y)
            def _():
                y_copy(d, part, other, other).wait_recv()
                total[start : start + size, :] += get_part(y_in.at[d, other], part)

        put_part(fins[d].at[space], part, total[start : start + size, :])

        def send(i, carry):
            gather_copy(d, part, lax.rem(z + order(i), nz), space).start()
            return carry

        lax.fori_loop(0, nz - 1, send, 0)

    def scan(d):
        for stage in (sum_z, scan_x, scan_y):
            for part in range(len(PARTS)):
                stage(d, part)
        forward_copy(d, z, space).start()

    def receive(d, off):
        j = lax.rem(z + off, nz)

        @pl.when(off != 0)
        def _():
            for part in range(len(PARTS)):
                gather_copy(d, part, j, at_z(j)).wait_recv()
            forward_copy(d, j, at_z(j)).start()

    def receive_pair(d, off):
        j = lax.rem(z + off, nz)
        forward_copy(d, j, 2 * j + 1 - core).wait_recv()

    def arrival(n):
        return jnp.where(n == 0, 0, order(n - 1))

    load(0, k_hbm, k_v).wait()
    load(1, v_hbm, v_v).wait()

    def state_of(head):
        keys, values = k_v[:, cols(head)], v_v[:, cols(head)]
        feat = jnp.maximum(keys, jnp.zeros_like(keys))
        return (
            across(feat, values),
            jnp.sum(feat.astype(F32), axis=0, keepdims=True),
            jnp.sum(values.astype(F32), axis=0, keepdims=True),
        )

    def pair_step(j, carry):
        put_state(pair_out.at[0, j], *state_of(2 * j + 1 - core))
        return carry

    lax.fori_loop(0, nz, pair_step, 0)
    pl.semaphore_wait(barrier, 1 + (nz - 1) + (nx - 1) + (ny - 1))

    def pair_send(i, carry):
        pair_copy(0, lax.rem(z + order(i), nz)).start()
        return carry

    lax.fori_loop(0, nz, pair_send, 0)

    def own_step(i, carry):
        off = order(i)
        j = lax.rem(z + off, nz)
        keep_own(j, state_of(at_z(j)))
        to_owner(0, off, 1)
        return carry

    lax.fori_loop(0, nz, own_step, 0)

    def rest_send(i, carry):
        for part in range(1, len(PARTS)):
            z_copy(0, part, lax.rem(z + order(i), nz), z).start()
        return carry

    lax.fori_loop(0, nz - 1, rest_send, 0)
    load(2, q_hbm, q_v).wait()
    load(3, g_hbm, g_v).wait()
    scan(0)

    count = ((tm + 1) * (rows * 2 * nz)).astype(F32)

    def attend(head):
        here = cols(head)
        queries, grad = q_v[:, here], g_v[:, here].astype(F32)
        feat = jnp.maximum(queries, jnp.zeros_like(queries))
        feat32 = feat.astype(F32)
        key_row, value_row = split_sums(fin0[head, D:STATE, :].astype(F32))
        numer = times(feat, fin0[head, 0:D, :]) + value_row
        denom = jnp.sum(feat32 * key_row, axis=1, keepdims=True) + count
        inverse = 1.0 / denom
        att_v[:, here] = (numer * inverse).astype(BF16)
        dnum = grad * inverse
        dnum_round = dnum.astype(BF16)
        dnum_v[:, here] = dnum_round
        ratio = jnp.sum(grad * numer, axis=1, keepdims=True) * (inverse * inverse)
        ratio_v[head] = ratio
        return (
            across(feat, dnum_round),
            -jnp.sum(ratio * feat32, axis=0, keepdims=True),
            jnp.sum(dnum, axis=0, keepdims=True),
        )

    def attend_step(n, carry):
        @pl.when(n < nz)
        def _():
            off = arrival(n)
            receive(0, off)
            j = lax.rem(z + off, nz)
            keep_own(j, attend(at_z(j)))

        @pl.when((n >= LAG) & (n < nz + LAG))
        def _():
            off = arrival(n - LAG)
            receive_pair(0, off)
            j = lax.rem(z + off, nz)
            give_pair(1, j, attend(2 * j + 1 - core))

        @pl.when(n >= 2 * LAG)
        def _():
            to_owner(1, arrival(n - 2 * LAG), len(PARTS))

        return carry

    lax.fori_loop(0, nz + 2 * LAG, attend_step, 0)

    def query_step(head, carry):
        here = cols(head)
        key_row, _ = split_sums(fin0[head, D:STATE, :].astype(F32))
        d_feat = times_t(dnum_v[:, here], fin0[head, 0:D, :]) - ratio_v[head] * key_row
        gq_v[:, here] = jnp.where(q_v[:, here].astype(F32) > 0, d_feat, 0.0).astype(BF16)
        return carry

    lax.fori_loop(0, 2 * nz, query_step, 0)
    scan(1)

    def key_value(head):
        here = cols(head)
        keys, values = k_v[:, here], v_v[:, here]
        feat = jnp.maximum(keys, jnp.zeros_like(keys))
        matrix = fin1[head, 0:D, :]
        key_row, value_row = split_sums(fin1[head, D:STATE, :].astype(F32))
        gv_v[:, here] = (times(feat, matrix) + value_row).astype(BF16)
        d_key = times_t(values, matrix) + key_row
        gk_v[:, here] = jnp.where(keys.astype(F32) > 0, d_key, 0.0).astype(BF16)

    def grads_step(n, carry):
        @pl.when(n < nz)
        def _():
            off = arrival(n)
            receive(1, off)
            key_value(at_z(lax.rem(z + off, nz)))

        @pl.when(n >= LAG)
        def _():
            off = arrival(n - LAG)
            receive_pair(1, off)
            key_value(2 * lax.rem(z + off, nz) + 1 - core)

        return carry

    lax.fori_loop(0, nz + LAG, grads_step, 0)

    for d in (0, 1):

        def sent(i, carry):
            off = order(i)
            j = lax.rem(z + off, nz)
            pair_copy(d, j).wait_send()
            forward_copy(d, j, at_z(j)).wait_send()

            @pl.when(off != 0)
            def _():
                for part in range(len(PARTS)):
                    z_copy(d, part, j, z).wait_send()
                    gather_copy(d, part, j, space).wait_send()

            return carry

        lax.fori_loop(0, nz, sent, 0)
        for o in range(1, nx):
            for part in range(len(PARTS)):
                x_copy(d, part, lax.rem(x + o, nx), x).wait_send()
        for o in range(1, ny):
            other = lax.rem(y + o, ny)

            @pl.when(other > y if d == 0 else other < y)
            def _():
                for part in range(len(PARTS)):
                    y_copy(d, part, other, y).wait_send()


def store_kernel(*refs):
    count = (len(refs) - 1) // 2
    sources, targets, sem = refs[:count], refs[count : 2 * count], refs[-1]
    half = sources[0].shape[0] // 2
    copies = [
        pltpu.make_async_copy(src.at[pl.ds(part * half, half)], dst.at[pl.ds(part * half, half)], sem.at[n, part])
        for n, (src, dst) in enumerate(zip(sources, targets))
        for part in range(2)
    ]
    for copy in copies:
        copy.start()
    for copy in copies:
        copy.wait()


def body(sizes, queries, keys, values, cotangent):
    nx, ny, nz = sizes
    heads = 2 * nz
    rows, width = queries.shape
    whole = pltpu.VMEM((rows, width), BF16)
    dma = pltpu.SemaphoreType.DMA
    like = jax.ShapeDtypeStruct((rows, width), BF16)
    in_vmem = pl.BlockSpec(memory_space=pltpu.VMEM)
    in_hbm = pl.BlockSpec(memory_space=pl.ANY)
    held = pl.pallas_call(
        functools.partial(kernel, sizes),
        out_shape=(whole,) * 4,
        in_specs=[pl.BlockSpec(memory_space=pltpu.HBM)] * 4,
        out_specs=(in_vmem,) * 4,
        scratch_shapes=[whole] * 5
        + [
            pltpu.VMEM((heads, rows, 1), F32),
            pltpu.VMEM((nz, STATE, D), F32),
            pltpu.VMEM((2, nz, STATE, D), BF16),
            pltpu.VMEM((2, nz, STATE, D), BF16),
            pltpu.VMEM((2, nz, STATE, D), BF16),
            pltpu.VMEM((2, nz, STATE, D), BF16),
            pltpu.VMEM((2, STATE, D), BF16),
            pltpu.VMEM((2, nx, STATE, D), BF16),
            pltpu.VMEM((2, STATE, D), BF16),
            pltpu.VMEM((2, ny, STATE, D), BF16),
            pltpu.VMEM((STATE, D), F32),
            pltpu.VMEM((heads, STATE, D), BF16),
            pltpu.VMEM((heads, STATE, D), BF16),
            dma((4,)),
            dma((2, nz)),
            dma((2, nz)),
            dma((2, 2, nz)),
            dma((2, 2, nz)),
            dma((2, 2, nx)),
            dma((2, 2, nx)),
            dma((2, 2, ny)),
            dma((2, 2, ny)),
            dma((2, 2, nz)),
            dma((2, 2, heads)),
            dma((2, nz)),
            dma((2, heads)),
        ],
        compiler_params=pltpu.CompilerParams(
            collective_id=0, has_side_effects=True, vmem_limit_bytes=32 << 20
        ),
        name="scan_attention",
    )(*(pltpu.with_memory_space_constraint(a, pltpu.HBM) for a in (queries, keys, values, cotangent)))
    return pl.pallas_call(
        store_kernel,
        out_shape=(like,) * 4,
        in_specs=[in_vmem] * 4,
        out_specs=(in_hbm,) * 4,
        scratch_shapes=[dma((4, 2))],
        compiler_params=pltpu.CompilerParams(vmem_limit_bytes=16 << 20),
        name="store",
    )(*held)


def solution(mesh):
    nz = mesh.shape["space"] // 2
    nx = int(round(mesh.shape["tm"] ** 0.5))
    ny = mesh.shape["tm"] // nx
    spec = P(("tm", "space"), None)
    return jax.shard_map(
        functools.partial(body, (nx, ny, nz)),
        mesh=mesh,
        in_specs=(spec,) * 4,
        out_specs=(spec,) * 4,
        check_vma=False,
    )
```
